256 devices in a mesh: out: 32 (over x, z_hi, core), in: 8 (over z_lo, y).
Axes of the slice: x: 4, y: 4, z: 8 (z_hi: 4, z_lo: 2; z = z_hi * 2 + z_lo), core: 2. Of those that a mesh axis runs over, the one named last changes fastest.
Arguments:
- slopes: bfloat16 [256, 163840], P('out', 'in'), may hold values from -6 to 6
- cols_first: int32 [128, 64], P(None, 'in'), may hold values from 0 to 79
- count_first: int32 [128, 8], P('out', 'in'), may hold values from 1 to 8
- weight_first: bfloat16 [128, 64, 256, 256], P('out', 'in'), may hold values from -0.0625 to 0.0625
- bias_first: float32 [32768], P(('out', 'in')), may hold values from -3 to 3
- cols_second: int32 [128, 32], P('out', 'in'), may hold values from 0 to 15
- count_second: int32 [128, 8], P('out', 'in'), may hold values from 1 to 4
- weight_second: bfloat16 [128, 32, 256, 256], P('out', 'in'), may hold values from -0.09375 to 0.09375
- bias_second: float32 [32768], P(('out', 'in')), may hold values from -3 to 3
- cotangent: bfloat16 [256, 32768], P(None, ('out', 'in')), may hold values from -6 to 6
Outputs:
- estimate: bfloat16 [256, 32768], P(None, ('out', 'in'))
- grad_first: bfloat16 [128, 64, 256, 256], P('out', 'in')
- grad_second: bfloat16 [128, 32, 256, 256], P('out', 'in')
The draws below stay inside these ranges and needn't reach their ends.
Inputs may be any that keep to these rules, and one draw needn't show every extreme that they name: `cols_first`: A local block index within the range of slopes of the slot's in index. `count_first`: slots of a block row at or after this count, within one in range, are not used. `cols_second`: A local block index within the range of reordered hidden units of the slot's in index. `count_second`: slots of a block row at or after this count, within one in range, are not used.
All inputs are finite; a program needn't handle non-finite values.
Results may differ from the reference program's by a relative error of at most 0.025.
Values may be sent and summed in bfloat16 or wider, within the bound.
No kernel may reach another device: no remote copies, remote signals or barrier semaphores. Data moves between devices by JAX's collectives and lax.ppermute only.
A program may use at most 128 MiB of HBM per device.

```python
import jax
import jax.numpy as jnp
from jax import lax

SLOPES = 163840
HIDDEN_SIZE = 32768
BLK = 256
KD1 = 8
KD2 = 4
FRAMES = 256
HB = 128
CB1 = 80
CB2 = 16
SUB = 128
N_OUT = 32
N_IN = 8


def plant(drawn, key, least, top_value):
    longest = drawn.shape.index(max(drawn.shape))
    spots = []
    for shift in (0, 1):
        where = [jax.random.randint(jax.random.fold_in(key, axis), (), 0, length) for axis, length in enumerate(drawn.shape)]
        where[longest] = (where[longest] + shift) % drawn.shape[longest]
        spots.append(tuple(where))
    return drawn.at[spots[0]].set(least).at[spots[1]].set(top_value)


def shard_levels(own_key, extent, pieces, smallest, top_value):
    gain, own = 1.0, jax.random.fold_in(own_key, 6)
    for dim, blocks in pieces:
        draws = jnp.exp(jax.random.uniform(jax.random.fold_in(own, dim), (blocks,), jnp.float32, smallest / len(pieces), top_value / len(pieces)))
        gain = gain * jnp.repeat(draws, extent[dim] // blocks).reshape([-1 if axis == dim else 1 for axis in range(len(extent))])
    return gain


def centred(own_key, extent, scale, most, pieces=(), kind=jnp.bfloat16):
    drawn = scale * jax.random.normal(own_key, extent, jnp.float32)
    if pieces:
        drawn = drawn * shard_levels(own_key, extent, pieces, -0.22, 0.18)
    return jnp.clip(drawn, -most, most).astype(kind)


def setup_inputs(seed: int = 0) -> dict:
    splits = jax.random.split(jax.random.key(seed), 11)
    return {
        "slopes": centred(splits[0], (FRAMES, SLOPES), 1.0, 6.0, ((0, 32), (1, 8))),
        "cols_first": plant(jax.random.randint(splits[1], (HB, N_IN * KD1), 0, CB1), jax.random.fold_in(splits[1], 1), 0, CB1 - 1).astype(jnp.int32),
        "count_first": plant(jax.random.randint(splits[2], (HB, N_IN), 1, KD1 + 1), jax.random.fold_in(splits[2], 1), 1, KD1).astype(jnp.int32),
        "weight_first": centred(splits[3], (HB, N_IN * KD1, BLK, BLK), (BLK * N_IN * KD1 // 2) ** -0.5, 0.0625, ((0, 32), (1, 8))),
        "bias_first": centred(splits[4], (HIDDEN_SIZE,), 0.5, 3.0, ((0, 256),), jnp.float32),
        "cols_second": plant(jax.random.randint(splits[5], (HB, N_IN * KD2), 0, CB2), jax.random.fold_in(splits[5], 1), 0, CB2 - 1).astype(jnp.int32),
        "count_second": plant(jax.random.randint(splits[6], (HB, N_IN), 1, KD2 + 1), jax.random.fold_in(splits[6], 1), 1, KD2).astype(jnp.int32),
        "weight_second": centred(splits[7], (HB, N_IN * KD2, BLK, BLK), (BLK * N_IN * KD2 // 2) ** -0.5, 0.09375, ((0, 32), (1, 8))),
        "bias_second": centred(splits[8], (HIDDEN_SIZE,), 0.5, 3.0, ((0, 256),), jnp.float32),
        "cotangent": centred(splits[9], (FRAMES, HIDDEN_SIZE), 1.0, 6.0, ((1, 256),)),
    }


def live_mask(counts, slots):
    column = jnp.arange(counts.shape[1] * slots, dtype=jnp.int32)
    spread = jnp.repeat(counts, slots, axis=1)
    return (column[None, :] % slots < spread).astype(jnp.float32)

def block_index(cols, blocks, slots):
    column = jnp.arange(cols.shape[1], dtype=jnp.int32)
    return ((column // slots)[None, :] * blocks + cols).astype(jnp.int32)

def to_second(values):
    return values.reshape(FRAMES, N_OUT, N_IN, SUB).transpose(0, 2, 1, 3).reshape(FRAMES, HIDDEN_SIZE)

def from_second(values):
    return values.reshape(FRAMES, N_IN, N_OUT, SUB).transpose(0, 2, 1, 3).reshape(FRAMES, HIDDEN_SIZE)

def layer_forward(inputs, index, weights, live, bias):
    blocks = inputs.reshape(FRAMES, -1, BLK)

    def one_row(operands):
        row_index, row_weight, row_live = operands
        taken = jnp.take(blocks, row_index, axis=1).astype(jnp.float32)
        masked = row_weight.astype(jnp.float32) * row_live[:, None, None]
        return jnp.einsum('fkb,kbo->fo', taken, masked)
    rows = lax.map(one_row, (index, weights, live))
    return jnp.transpose(rows, (1, 0, 2)).reshape(FRAMES, HIDDEN_SIZE) + bias[None, :]

def layer_weight_grad(inputs, index, live, delta):
    blocks = inputs.reshape(FRAMES, -1, BLK)
    delta_rows = jnp.transpose(delta.reshape(FRAMES, HB, BLK), (1, 0, 2))

    def one_row(operands):
        row_index, row_live, row_delta = operands
        taken = jnp.take(blocks, row_index, axis=1).astype(jnp.float32)
        grad = jnp.einsum('fkb,fo->kbo', taken, row_delta.astype(jnp.float32))
        return (grad * row_live[:, None, None]).astype(jnp.bfloat16)
    return lax.map(one_row, (index, live, delta_rows))

def layer_adjoint(index, weights, live, delta, width):
    delta_rows = jnp.transpose(delta.reshape(FRAMES, HB, BLK), (1, 0, 2))

    def one_row(total, operands):
        row_index, row_weight, row_live, row_delta = operands
        masked = row_weight.astype(jnp.float32) * row_live[:, None, None]
        term = jnp.einsum('fo,kbo->fkb', row_delta.astype(jnp.float32), masked)
        return (total.at[:, row_index, :].add(term), None)
    start = jnp.zeros((FRAMES, width // BLK, BLK), jnp.float32)
    total, unused = lax.scan(one_row, start, (index, weights, live, delta_rows))
    return total.reshape(FRAMES, width)

def reference(slopes, cols_first, count_first, weight_first, bias_first, cols_second, count_second, weight_second, bias_second, cotangent):
    live_first = live_mask(count_first, KD1)
    live_second = live_mask(count_second, KD2)
    index_first = block_index(cols_first, CB1, KD1)
    index_second = block_index(cols_second, CB2, KD2)
    hidden_first = jnp.tanh(layer_forward(slopes, index_first, weight_first, live_first, bias_first)).astype(jnp.bfloat16)
    ordered = to_second(hidden_first)
    estimate = jnp.tanh(layer_forward(ordered, index_second, weight_second, live_second, bias_second)).astype(jnp.bfloat16)
    est32 = estimate.astype(jnp.float32)
    delta_second = (cotangent.astype(jnp.float32) * (1.0 - est32 * est32)).astype(jnp.bfloat16)
    grad_second = layer_weight_grad(ordered, index_second, live_second, delta_second)
    back_ordered = layer_adjoint(index_second, weight_second, live_second, delta_second, HIDDEN_SIZE)
    back_first = from_second(back_ordered)
    hid32 = hidden_first.astype(jnp.float32)
    delta_first = (back_first * (1.0 - hid32 * hid32)).astype(jnp.bfloat16)
    grad_first = layer_weight_grad(slopes, index_first, live_first, delta_first)
    return (estimate, grad_first, grad_second)
```

```python
import jax
import jax.numpy as jnp
from jax import lax
from jax.experimental import pallas as pl
from jax.experimental.pallas import tpu as pltpu
from jax.sharding import Mesh
from jax.sharding import PartitionSpec as P

BLK = 256
KD1 = 8
KD2 = 4
SUB = 128
OUT = ("x", "zh", "core")
IN = ("zl", "y")
F32 = jnp.float32
BF16 = jnp.bfloat16


def dot(a, b, dims):
    return lax.dot_general(a, b, (dims, ((), ())), preferred_element_type=F32)


def forward_first(gathered, weight, cols, count):
    frames = gathered.shape[0]
    rows = weight.shape[0]

    def body(cols_ref, count_ref, *refs):
        panels, w_ref, out_ref, acc = refs[:KD1], refs[KD1], refs[KD1 + 1], refs[KD1 + 2]
        r = pl.program_id(0)
        acc[...] = dot(panels[0][...], w_ref[0, 0], ((1,), (0,)))
        for k in range(1, KD1):

            @pl.when(k < count_ref[r])
            def _():
                acc[...] += dot(panels[k][...], w_ref[0, k], ((1,), (0,)))

        out_ref[0] = acc[:, :SUB].astype(BF16)
        out_ref[1] = acc[:, SUB:].astype(BF16)

    return pl.pallas_call(
        body,
        out_shape=jax.ShapeDtypeStruct((rows * BLK // SUB, frames, SUB), BF16),
        grid_spec=pltpu.PrefetchScalarGridSpec(
            num_scalar_prefetch=2,
            grid=(rows,),
            in_specs=[
                pl.BlockSpec((frames, BLK), lambda r, cols, count, k=k: (0, cols[r, k]))
                for k in range(KD1)
            ]
            + [pl.BlockSpec((1, KD1, BLK, BLK), lambda r, cols, count: (r, 0, 0, 0))],
            out_specs=pl.BlockSpec((BLK // SUB, frames, SUB), lambda r, cols, count: (r, 0, 0)),
            scratch_shapes=[pltpu.VMEM((frames, BLK), F32)],
        ),
        name="forward_first",
    )(cols, count, *([gathered] * KD1), weight)


def grad_first_blocks(gathered, delta, cols, count):
    frames = gathered.shape[0]
    rows = cols.shape[0]

    def body(cols_ref, count_ref, *refs):
        panels, d_ref, out_ref = refs[:KD1], refs[KD1], refs[KD1 + 1]
        r = pl.program_id(0)
        d = jnp.concatenate([d_ref[0], d_ref[1]], axis=1)
        for k in range(KD1):

            @pl.when(k < count_ref[r])
            def _():
                out_ref[0, k] = dot(panels[k][...], d, ((0,), (0,))).astype(BF16)

            @pl.when(k >= count_ref[r])
            def _():
                out_ref[0, k] = jnp.zeros((BLK, BLK), BF16)

    return pl.pallas_call(
        body,
        out_shape=jax.ShapeDtypeStruct((rows, KD1, BLK, BLK), BF16),
        grid_spec=pltpu.PrefetchScalarGridSpec(
            num_scalar_prefetch=2,
            grid=(rows,),
            in_specs=[
                pl.BlockSpec((frames, BLK), lambda r, cols, count, k=k: (0, cols[r, k]))
                for k in range(KD1)
            ]
            + [pl.BlockSpec((BLK // SUB, frames, SUB), lambda r, cols, count: (r, 0, 0))],
            out_specs=pl.BlockSpec((1, KD1, BLK, BLK), lambda r, cols, count: (r, 0, 0, 0)),
        ),
        name="grad_first",
    )(cols, count, *([gathered] * KD1), delta)


def forward_second(hidden, weight, cols, count):
    frames = hidden.shape[1]
    rows = weight.shape[0]
    per = BLK // SUB

    def body(cols_ref, count_ref, h_ref, w_ref, out_ref, acc):
        for r in range(rows):
            for k in range(KD2):

                def term(r=r, k=k):
                    c = cols_ref[r, k]
                    block = jnp.concatenate([h_ref[per * c], h_ref[per * c + 1]], axis=1)
                    return dot(block, w_ref[r, k], ((1,), (0,)))

                if k == 0:
                    acc[...] = term()
                else:

                    @pl.when(k < count_ref[r])
                    def _():
                        acc[...] += term()

            out_ref[per * r] = acc[:, :SUB].astype(BF16)
            out_ref[per * r + 1] = acc[:, SUB:].astype(BF16)

    return pl.pallas_call(
        body,
        out_shape=jax.ShapeDtypeStruct((rows * per, frames, SUB), BF16),
        in_specs=[
            pl.BlockSpec(memory_space=pltpu.SMEM),
            pl.BlockSpec(memory_space=pltpu.SMEM),
            pl.BlockSpec(memory_space=pltpu.VMEM),
            pl.BlockSpec(memory_space=pltpu.VMEM),
        ],
        out_specs=pl.BlockSpec(memory_space=pltpu.VMEM),
        scratch_shapes=[pltpu.VMEM((frames, BLK), F32)],
        name="forward_second",
    )(cols, count, hidden, weight)


def adjoint_second(delta, weight, cols, count, blocks):
    frames = delta.shape[1]
    rows = weight.shape[0]
    per = BLK // SUB

    def body(cols_ref, count_ref, d_ref, w_ref, out_ref, acc):
        acc[...] = jnp.zeros(acc.shape, F32)
        for r in range(rows):
            d = jnp.concatenate([d_ref[per * r], d_ref[per * r + 1]], axis=1)
            for k in range(KD2):

                @pl.when(k < count_ref[r])
                def _():
                    c = cols_ref[r, k]
                    acc[c] += dot(d, w_ref[r, k], ((1,), (1,)))

        for c in range(blocks):
            out_ref[per * c] = acc[c, :, :SUB].astype(BF16)
            out_ref[per * c + 1] = acc[c, :, SUB:].astype(BF16)

    return pl.pallas_call(
        body,
        out_shape=jax.ShapeDtypeStruct((blocks * per, frames, SUB), BF16),
        in_specs=[
            pl.BlockSpec(memory_space=pltpu.SMEM),
            pl.BlockSpec(memory_space=pltpu.SMEM),
            pl.BlockSpec(memory_space=pltpu.VMEM),
            pl.BlockSpec(memory_space=pltpu.VMEM),
        ],
        out_specs=pl.BlockSpec(memory_space=pltpu.VMEM),
        scratch_shapes=[pltpu.VMEM((blocks, frames, BLK), F32)],
        name="adjoint_second",
    )(cols, count, delta, weight)


def grad_second_blocks(hidden, delta, cols, count):
    frames = hidden.shape[1]
    rows = cols.shape[0]
    per = BLK // SUB

    def body(cols_ref, count_ref, h_ref, d_ref, out_ref):
        for r in range(rows):
            d = jnp.concatenate([d_ref[per * r], d_ref[per * r + 1]], axis=1)
            for k in range(KD2):

                @pl.when(k < count_ref[r])
                def _():
                    c = cols_ref[r, k]
                    block = jnp.concatenate([h_ref[per * c], h_ref[per * c + 1]], axis=1)
                    out_ref[r, k] = dot(block, d, ((0,), (0,))).astype(BF16)

                @pl.when(k >= count_ref[r])
                def _():
                    out_ref[r, k] = jnp.zeros((BLK, BLK), BF16)

    return pl.pallas_call(
        body,
        out_shape=jax.ShapeDtypeStruct((rows, KD2, BLK, BLK), BF16),
        in_specs=[
            pl.BlockSpec(memory_space=pltpu.SMEM),
            pl.BlockSpec(memory_space=pltpu.SMEM),
            pl.BlockSpec(memory_space=pltpu.VMEM),
            pl.BlockSpec(memory_space=pltpu.VMEM),
        ],
        out_specs=pl.BlockSpec(memory_space=pltpu.VMEM),
        name="grad_second",
    )(cols, count, hidden, delta)


def shards(
    slopes,
    cols_first,
    count_first,
    weight_first,
    bias_first,
    cols_second,
    count_second,
    weight_second,
    bias_second,
    cotangent,
):
    rows = weight_first.shape[0]
    out_at = lax.axis_index(OUT)
    own_cols = lax.dynamic_slice_in_dim(cols_first, out_at * rows, rows, 0)
    live_first = count_first[:, 0]
    live_second = count_second[:, 0]
    gathered = lax.all_gather(slopes, OUT, axis=0, tiled=True)

    partial_first = forward_first(gathered, weight_first, own_cols, live_first)
    parts_first = lax.all_to_all(partial_first, IN, 0, 0, tiled=True)
    summed_first = jnp.sum(parts_first.astype(F32), axis=0)
    hidden_first = jnp.tanh(summed_first + bias_first[None, :]).astype(BF16)
    hidden = lax.all_gather(hidden_first, OUT, axis=0)

    partial_second = forward_second(hidden, weight_second, cols_second, live_second)
    parts_second = lax.all_to_all(partial_second, IN, 0, 0, tiled=True)
    summed_second = jnp.sum(parts_second.astype(F32), axis=0)
    estimate = jnp.tanh(summed_second + bias_second[None, :]).astype(BF16)
    est32 = estimate.astype(F32)
    delta_second = (cotangent.astype(F32) * (1.0 - est32 * est32)).astype(BF16)
    rows_second = lax.all_gather(delta_second, IN, axis=0)

    back = adjoint_second(rows_second, weight_second, cols_second, live_second, hidden.shape[0] // 2)
    parts_back = lax.all_to_all(back, OUT, 0, 0, tiled=True)
    back_first = jnp.sum(parts_back.astype(F32), axis=0)
    hid32 = hidden_first.astype(F32)
    delta_first = (back_first * (1.0 - hid32 * hid32)).astype(BF16)
    rows_first = lax.all_gather(delta_first, IN, axis=0)
    grad_second = grad_second_blocks(hidden, rows_second, cols_second, live_second)
    grad_first = grad_first_blocks(gathered, rows_first, own_cols, live_first)
    return (estimate, grad_first, grad_second)


def solution(mesh):
    fine = Mesh(mesh.devices.reshape(4, 4, 2, 2, 4), OUT + IN)
    return jax.shard_map(
        shards,
        mesh=fine,
        in_specs=(
            P(OUT, IN),
            P(None, IN),
            P(OUT, IN),
            P(OUT, IN, None, None),
            P(OUT + IN),
            P(OUT, IN),
            P(OUT, IN),
            P(OUT, IN, None, None),
            P(OUT + IN),
            P(None, OUT + IN),
        ),
        out_specs=(P(None, OUT + IN), P(OUT, IN, None, None), P(OUT, IN, None, None)),
        check_vma=False,
    )
```

```python
import jax
import jax.numpy as jnp
from jax import lax
from jax.experimental import pallas as pl
from jax.experimental.pallas import tpu as pltpu
from jax.sharding import Mesh
from jax.sharding import PartitionSpec as P

BLK = 256
KD1 = 8
KD2 = 4
SUB = 128
ROWS = 4
NX = 4
NZ = 4
OUT = ("x", "zh", "core")
IN = ("zl", "y")
F32 = jnp.float32
BF16 = jnp.bfloat16

HBM = pl.BlockSpec(memory_space=pltpu.HBM)
SMEM = pl.BlockSpec(memory_space=pltpu.SMEM)
VMEM = pl.BlockSpec(memory_space=pltpu.VMEM)


def dot(a, b, dims):
    return lax.dot_general(a, b, (dims, ((), ())), preferred_element_type=F32)


def halves(ref, row, *at):
    return jnp.concatenate([ref[(2 * row, *at)], ref[(2 * row + 1, *at)]], axis=1)


def limit(mib):
    return pltpu.CompilerParams(vmem_limit_bytes=mib * 2**20)


def on_chip(*values):
    return [pltpu.with_memory_space_constraint(v, pltpu.VMEM) for v in values]


def in_hbm(*values):
    return [pltpu.with_memory_space_constraint(v, pltpu.HBM) for v in values]


def forward_first(pos, cols, table, sib_table, pieces, weight, sibling):
    arrays = [a for a, _, _ in pieces]
    n = len(arrays)
    own_rows = arrays[0].shape[0]
    width = arrays[0].shape[1]
    frames = NX * NZ * own_rows
    n_copies = sum(len(o) for _, o, _ in pieces)

    def body(pos_ref, cols_ref, tab_ref, sib_tab_ref, *refs):
        srcs, (own_ref, sib_ref, out_ref, p_own, p_sib) = refs[:n], refs[n : n + 5]
        whole, weights, sems, wsems, psems = refs[n + 5 :]
        x, z, core, out_at = pos_ref[0], pos_ref[1], pos_ref[2], pos_ref[3]
        copies = []
        for src, (a, offsets, first) in zip(srcs, pieces):
            for m, (dx, dz) in enumerate(offsets):
                row = ((x + dx) % NX * NZ + (z + dz) % NZ) * own_rows
                copies.append(
                    pltpu.make_async_copy(
                        src.at[pl.ds(m * own_rows, own_rows), :],
                        whole.at[
                            pl.ds(pl.multiple_of(row, own_rows), own_rows),
                            pl.ds(first, a.shape[1]),
                        ],
                        sems.at[len(copies)],
                    )
                )
                copies[-1].start()

        def load(who, r):
            src = (own_ref, sib_ref)[who]
            return pltpu.make_async_copy(src.at[r], weights.at[who, r], wsems.at[who, r])

        for who in range(2):
            for r in range(ROWS):
                load(who, r).start()
        for c in copies:
            c.wait()
        for mine in (True, False):
            who, tab, to = (0, tab_ref, p_own) if mine else (1, sib_tab_ref, p_sib)
            base = (out_at if mine else out_at ^ 1) * ROWS
            side = core if mine else 1 - core
            sem = psems.at[who]

            def row(r, _, who=who, base=base, side=side, tab=tab, to=to, sem=sem):
                panels = []
                for k in range(KD1):
                    at = pl.ds(pl.multiple_of(cols_ref[base + r, k] * BLK, BLK), BLK)
                    pltpu.make_async_copy(whole.at[:, at], to.at[r, k], sem).start()
                    panels.append(whole[:, at] * (k < tab[r, 0]).astype(BF16))
                load(who, r).wait()
                weight = weights[who, r].reshape(KD1 * BLK, BLK)
                out = dot(jnp.concatenate(panels, axis=1), weight, ((1,), (0,)))
                out_ref[2 * r, side] = out[:, :SUB].astype(BF16)
                out_ref[2 * r + 1, side] = out[:, SUB:].astype(BF16)
                return 0

            lax.fori_loop(0, ROWS, row, 0)
        for mine in (True, False):
            to = p_own if mine else p_sib
            pltpu.make_async_copy(to, to, psems.at[0 if mine else 1]).wait()

    panels = pltpu.HBM((ROWS, KD1, frames, BLK), BF16)
    return pl.pallas_call(
        body,
        out_shape=(jax.ShapeDtypeStruct((2 * ROWS, 2, frames, SUB), BF16), panels, panels),
        in_specs=[SMEM] * 4 + [HBM] * (n + 2),
        out_specs=(VMEM, HBM, HBM),
        scratch_shapes=[
            pltpu.VMEM((frames, width), BF16),
            pltpu.VMEM((2, ROWS, KD1, BLK, BLK), BF16),
            pltpu.SemaphoreType.DMA((n_copies,)),
            pltpu.SemaphoreType.DMA((2, ROWS)),
            pltpu.SemaphoreType.DMA((2,)),
        ],
        compiler_params=limit(20),
        cost_estimate=pl.CostEstimate(flops=2**31, bytes_accessed=2**24, transcendentals=0),
        name="forward_first",
    )(pos, cols, table, sib_table, *in_hbm(*arrays, weight, sibling))


def relative(block, x, z):
    return (block // NZ - x) % NX * NZ + (block % NZ - z) % NZ


def forward_second(pos, table, sib_table, pieces, weight, sibling):
    frames = pieces[0].shape[2]

    def body(pos_ref, tab_ref, sib_tab_ref, *refs):
        srcs, (own_ref, sib_ref, out_ref, p_own, p_sib) = refs[:NX], refs[NX : NX + 5]
        blocks, panels, psems = refs[NX + 5 :]
        x, z, core = pos_ref[0], pos_ref[1], pos_ref[2]
        for k in range(NX):
            for zr in range(NZ):
                blocks[k * NZ + zr, :, :SUB] = srcs[k][zr, 0]
                blocks[k * NZ + zr, :, SUB:] = srcs[k][zr, 1]
        for mine in (True, False):
            w_ref, tab, to = (own_ref, tab_ref, p_own) if mine else (sib_ref, sib_tab_ref, p_sib)
            side = core if mine else 1 - core
            n = 0 if mine else 1

            def row(r, _):
                used = []
                for k in range(KD2):
                    panel = blocks[relative(tab[r, 2 + k], x, z)]
                    panels[n, r, k] = panel
                    used.append(panel * (k < tab[r, 1]).astype(BF16))
                pltpu.make_async_copy(panels.at[n, r], to.at[r], psems.at[n]).start()
                out = dot(jnp.concatenate(used, axis=1), w_ref[r].reshape(KD2 * BLK, BLK), ((1,), (0,)))
                out_ref[2 * r, side] = out[:, :SUB].astype(BF16)
                out_ref[2 * r + 1, side] = out[:, SUB:].astype(BF16)
                return 0

            lax.fori_loop(0, ROWS, row, 0)
        for n, to in enumerate((p_own, p_sib)):
            pltpu.make_async_copy(to, to, psems.at[n]).wait()

    panels = pltpu.HBM((ROWS, KD2, frames, BLK), BF16)
    return pl.pallas_call(
        body,
        out_shape=(jax.ShapeDtypeStruct((2 * ROWS, 2, frames, SUB), BF16), panels, panels),
        in_specs=[SMEM] * 3 + [VMEM] * (NX + 2),
        out_specs=(VMEM, HBM, HBM),
        scratch_shapes=[
            pltpu.VMEM((NX * NZ, frames, BLK), BF16),
            pltpu.VMEM((2, ROWS, KD2, frames, BLK), BF16),
            pltpu.SemaphoreType.DMA((2,)),
        ],
        compiler_params=limit(12),
        cost_estimate=pl.CostEstimate(flops=2**30, bytes_accessed=2**23, transcendentals=0),
        name="forward_second",
    )(pos, table, sib_table, *on_chip(*pieces, weight, sibling))


def adjoint_second(pos, table, sib_table, delta, weight, sibling):
    frames = delta.shape[2]

    def body(pos_ref, tab_ref, sib_tab_ref, d_ref, own_ref, sib_ref, *refs):
        outs, (acc,) = refs[:NX], refs[NX:]
        x, z, core = pos_ref[0], pos_ref[1], pos_ref[2]
        acc[...] = jnp.zeros(acc.shape, F32)
        for mine in (True, False):
            w_ref, tab = (own_ref, tab_ref) if mine else (sib_ref, sib_tab_ref)
            side = core if mine else 1 - core

            def row(r, _):
                d = halves(d_ref, r, side)
                terms = dot(d, w_ref[r].reshape(KD2 * BLK, BLK), ((1,), (1,)))
                for k in range(KD2):
                    term = terms[:, k * BLK : (k + 1) * BLK]
                    acc[relative(tab[r, 2 + k], x, z)] += term * (k < tab[r, 1]).astype(F32)
                return 0

            lax.fori_loop(0, ROWS, row, 0)
        for k in range(NX):
            for zr in range(NZ):
                outs[k][zr, 0] = acc[k * NZ + zr, :, :SUB].astype(BF16)
                outs[k][zr, 1] = acc[k * NZ + zr, :, SUB:].astype(BF16)

    return pl.pallas_call(
        body,
        out_shape=(jax.ShapeDtypeStruct((NZ, 2, frames, SUB), BF16),) * NX,
        in_specs=[SMEM] * 3 + [VMEM] * 3,
        out_specs=(VMEM,) * NX,
        scratch_shapes=[pltpu.VMEM((NX * NZ, frames, BLK), F32)],
        compiler_params=limit(12),
        cost_estimate=pl.CostEstimate(flops=2**30, bytes_accessed=2**23, transcendentals=0),
        name="adjoint_second",
    )(pos, table, sib_table, *on_chip(delta, weight, sibling))


def add_shares(parts):
    n = parts[0].shape[0]

    def body(*refs):
        ins, outs = refs[: len(parts)], refs[len(parts) :]
        for k in range(n):
            total = ins[0][k].astype(F32)
            for p in ins[1:]:
                total += p[k].astype(F32)
            outs[k][...] = total.astype(BF16)

    return pl.pallas_call(
        body,
        out_shape=(jax.ShapeDtypeStruct(parts[0].shape[1:], BF16),) * n,
        in_specs=[VMEM] * len(parts),
        out_specs=(VMEM,) * n,
        compiler_params=limit(8),
        name="add_shares",
    )(*on_chip(*parts))


def weight_grads(pos, table, field, panels, other_panels, deltas, name):
    arrays, rows_of = deltas
    slots, frames = panels.shape[1], panels.shape[2]

    def body(pos_ref, tab_ref, p_ref, po_ref, *refs):
        d_refs, (out_ref, grads, gsem) = refs[: len(arrays)], refs[len(arrays) :]
        core = pos_ref[2]

        def row(r, _):
            d = jnp.concatenate(rows_of(core, d_refs, r), axis=0)
            for k in range(slots):
                panel = jnp.concatenate([p_ref[r, k], po_ref[r, k]], axis=0)
                live = (k < tab_ref[r, field]).astype(F32)
                grads[r, k] = (dot(panel, d, ((0,), (0,))) * live).astype(BF16)
            pltpu.make_async_copy(grads.at[r], out_ref.at[r], gsem).start()
            return 0

        lax.fori_loop(0, ROWS, row, 0)
        pltpu.make_async_copy(out_ref, out_ref, gsem).wait()

    return pl.pallas_call(
        body,
        out_shape=jax.ShapeDtypeStruct((ROWS, slots, BLK, BLK), BF16),
        in_specs=[SMEM, SMEM] + [VMEM] * (2 + len(arrays)),
        out_specs=HBM,
        scratch_shapes=[
            pltpu.VMEM((ROWS, slots, BLK, BLK), BF16),
            pltpu.SemaphoreType.DMA,
        ],
        compiler_params=limit(12),
        cost_estimate=pl.CostEstimate(
            flops=slots * 2**27, bytes_accessed=slots * 2**20, transcendentals=0
        ),
        name=name,
    )(pos, table, *on_chip(panels, other_panels, *arrays))


def ring(value, axis, step, label="ring"):
    n = lax.axis_size(axis)
    with jax.named_scope("L_" + label):
        return lax.ppermute(value, axis, [(i, (i + step) % n) for i in range(n)])


def swap(value, label="swap"):
    with jax.named_scope("L_" + label):
        return lax.ppermute(value, "core", [(0, 1), (1, 0)])


def together(*values):
    return lax.optimization_barrier(values)


def gather_slopes(s):
    half = s.shape[1] // 2
    zp, zn = ring(s, "zh", 1, "zp"), ring(s, "zh", -1, "zn")
    xp, xn = ring(s, "x", 1, "xp"), ring(s, "x", -1, "xn")
    zp, zn, xp, xn = together(zp, zn, xp, xn)
    zps, zns = zp[:, :half], zn[:, half:]
    t = jnp.concatenate([zp, zn], axis=0)
    zps, zns, t = together(zps, zns, t)
    zl, zr = ring(zps, "zh", 1, "zl"), ring(zns, "zh", -1, "zr")
    tp, tn = ring(t, "x", 1, "tp"), ring(t, "x", -1, "tn")
    zl, zr = together(zl, zr)
    f = jnp.concatenate([zl, zr], axis=1)
    fp, fn = ring(f, "x", 1, "fp"), ring(f, "x", -1, "fn")
    tp, tn = together(tp, tn)
    ol = jnp.concatenate([xp[:, :half], tp[:, :half]], axis=0)
    oh = jnp.concatenate([xn[:, half:], tn[:, half:]], axis=0)
    ol, oh = ring(ol, "x", 1, "ol"), ring(oh, "x", -1, "oh")
    fp, fn = together(fp, fn)
    fl, fh = ring(fp[:, :half], "x", 1, "fl"), ring(fn[:, half:], "x", -1, "fh")
    pieces = [(s, [(0, 0)], 0), (xp, [(-1, 0)], 0), (xn, [(1, 0)], 0)]
    pieces += [(t, [(0, -1), (0, 1)], 0), (tp, [(-1, -1), (-1, 1)], 0), (tn, [(1, -1), (1, 1)], 0)]
    pieces += [(f, [(0, 2)], 0), (fp, [(-1, 2)], 0), (fn, [(1, 2)], 0)]
    pieces += [(a, [(2, 0), (2, -1), (2, 1)], first) for a, first in ((ol, 0), (oh, half))]
    pieces += [(fl, [(2, 2)], 0), (fh, [(2, 2)], half)]
    return pieces


def gather_axis(value, axis):
    n = lax.axis_size(axis)
    return lax.all_to_all(jnp.broadcast_to(value[None], (n, *value.shape)), axis, 0, 0, tiled=True)


def sum_axis(parts, axis):
    return jnp.sum(lax.all_to_all(parts, axis, 0, 0, tiled=True).astype(F32), axis=0)


def shards(
    slopes,
    cols_first,
    count_first,
    weight_first,
    bias_first,
    cols_second,
    count_second,
    weight_second,
    bias_second,
    cotangent,
):
    frames = cotangent.shape[0]
    chips = NX * NZ
    own = slopes.shape[0]
    core = lax.axis_index("core")
    pos = jnp.stack(
        [lax.axis_index("x"), lax.axis_index("zh"), core, lax.axis_index(OUT)]
    ).astype(jnp.int32)

    def canonical(mine, other):
        return jnp.where(core == 0, jnp.stack([mine, other]), jnp.stack([other, mine]))

    pieces = gather_slopes(slopes)
    sibling_first = swap(weight_first)
    sibling_second = swap(weight_second)
    table = jnp.concatenate([count_first, count_second, cols_second], axis=1)
    sib_table = swap(table)
    bias = jnp.stack([bias_first, bias_second])
    biases = canonical(bias, swap(bias))
    by_core = cotangent.reshape(chips, 2, own, SUB)
    mine = lax.dynamic_index_in_dim(by_core, core, 1, keepdims=False)
    theirs = lax.dynamic_index_in_dim(by_core, 1 - core, 1, keepdims=False)
    cot = canonical(mine, swap(theirs)).reshape(2, chips * own, SUB).astype(F32)

    partial_first, panels_first, lent_first = forward_first(
        pos, cols_first, table, sib_table, pieces, weight_first, sibling_first
    )
    summed_first = sum_axis(partial_first, IN)
    hidden_first = jnp.tanh(summed_first + biases[:, 0][:, None, :]).astype(BF16)
    along_z = jnp.stack([hidden_first] + [ring(hidden_first, "zh", -k) for k in range(1, NZ)])
    hidden = [along_z] + [ring(along_z, "x", -k) for k in range(1, NX)]

    partial_second, panels_second, lent_second = forward_second(
        pos, table, sib_table, hidden, weight_second, sibling_second
    )
    summed_second = sum_axis(partial_second, IN)
    estimate = jnp.tanh(summed_second + biases[:, 1][:, None, :]).astype(BF16)
    est32 = estimate.astype(F32)
    delta_second = (cot * (1.0 - est32 * est32)).astype(BF16)
    rows_second = gather_axis(delta_second, IN)

    back = adjoint_second(pos, table, sib_table, rows_second, weight_second, sibling_second)
    along_x = add_shares([back[0]] + [ring(back[k], "x", k) for k in range(1, NX)])
    shares = [along_x[0]] + [ring(along_x[k], "zh", k) for k in range(1, NZ)]
    back_first = sum(s.astype(F32) for s in shares)
    hid32 = hidden_first.astype(F32)
    delta_first = (back_first * (1.0 - hid32 * hid32)).astype(BF16)
    to_all = jnp.broadcast_to(delta_first[:, None], (2, lax.axis_size(IN), *delta_first.shape[1:]))
    rows_first = lax.all_to_all(
        to_all.reshape(-1, *delta_first.shape[1:]), ("core", *IN), 0, 0, tiled=True
    ).reshape(to_all.shape)
    lent_rows = swap(lax.dynamic_index_in_dim(rows_second, 1 - core, 1, keepdims=False))
    grad_second = weight_grads(
        pos,
        table,
        1,
        panels_second,
        swap(lent_second),
        (
            (rows_second, lent_rows),
            lambda core, refs, r: [halves(refs[0], r, core), halves(refs[1], r)],
        ),
        "grad_second",
    )
    est_own = lax.dynamic_index_in_dim(estimate, core, 0, keepdims=False)
    est_other = swap(lax.dynamic_index_in_dim(estimate, 1 - core, 0, keepdims=False))
    both = canonical(est_own, est_other).reshape(2, chips, own, SUB)
    estimate_out = both.transpose(1, 0, 2, 3).reshape(frames, SUB)
    rows_first, grad_second, estimate_out = together(rows_first, grad_second, estimate_out)
    grad_first = weight_grads(
        pos,
        table,
        0,
        panels_first,
        swap(lent_first),
        (
            (rows_first,),
            lambda core, refs, r: [halves(refs[0].at[core], r), halves(refs[0].at[1 - core], r)],
        ),
        "grad_first",
    )
    return (estimate_out, grad_first, grad_second)


def solution(mesh):
    fine = Mesh(mesh.devices.reshape(NX, NZ, 2, 2, 4), OUT + IN)
    return jax.shard_map(
        shards,
        mesh=fine,
        in_specs=(
            P(OUT, IN),
            P(None, IN),
            P(OUT, IN),
            P(OUT, IN, None, None),
            P(OUT + IN),
            P(OUT, IN),
            P(OUT, IN),
            P(OUT, IN, None, None),
            P(OUT + IN),
            P(None, OUT + IN),
        ),
        out_specs=(P(None, OUT + IN), P(OUT, IN, None, None), P(OUT, IN, None, None)),
        check_vma=False,
    )
```

```python
import jax
import jax.numpy as jnp
from jax import lax
from jax.experimental import pallas as pl
from jax.experimental.pallas import tpu as pltpu
from jax.sharding import Mesh
from jax.sharding import PartitionSpec as P

BLK = 256
KD1 = 8
KD2 = 4
SUB = 128
ROWS = 4
NX = 4
NZ = 4
OUT = ("x", "zh", "core")
IN = ("zl", "y")
F32 = jnp.float32
BF16 = jnp.bfloat16

HBM = pl.BlockSpec(memory_space=pltpu.HBM)
SMEM = pl.BlockSpec(memory_space=pltpu.SMEM)
VMEM = pl.BlockSpec(memory_space=pltpu.VMEM)


def dot(a, b, dims):
    return lax.dot_general(a, b, (dims, ((), ())), preferred_element_type=F32)


def halves(ref, row, *at):
    return jnp.concatenate([ref[(2 * row, *at)], ref[(2 * row + 1, *at)]], axis=1)


def limit(mib):
    return pltpu.CompilerParams(vmem_limit_bytes=mib * 2**20)


def on_chip(*values):
    return [pltpu.with_memory_space_constraint(v, pltpu.VMEM) for v in values]


def in_hbm(*values):
    return [pltpu.with_memory_space_constraint(v, pltpu.HBM) for v in values]


def forward_first(pos, cols, table, sib_table, pieces, weight, sibling):
    arrays = [a for a, _, _ in pieces]
    n = len(arrays)
    own_rows = arrays[0].shape[0]
    width = arrays[0].shape[1]
    frames = NX * NZ * own_rows
    n_copies = sum(len(o) for _, o, _ in pieces)

    def body(pos_ref, cols_ref, tab_ref, sib_tab_ref, *refs):
        srcs, (own_ref, sib_ref, out_ref, p_own, p_sib) = refs[:n], refs[n : n + 5]
        whole, weights, sems, wsems, psems = refs[n + 5 :]
        x, z, core, out_at = pos_ref[0], pos_ref[1], pos_ref[2], pos_ref[3]
        copies = []
        for src, (a, offsets, first) in zip(srcs, pieces):
            for m, (dx, dz) in enumerate(offsets):
                row = ((x + dx) % NX * NZ + (z + dz) % NZ) * own_rows
                copies.append(
                    pltpu.make_async_copy(
                        src.at[pl.ds(m * own_rows, own_rows), :],
                        whole.at[
                            pl.ds(pl.multiple_of(row, own_rows), own_rows),
                            pl.ds(first, a.shape[1]),
                        ],
                        sems.at[len(copies)],
                    )
                )
                copies[-1].start()

        def load(who, r):
            src = (own_ref, sib_ref)[who]
            return pltpu.make_async_copy(src.at[r], weights.at[who, r], wsems.at[who, r])

        for who in range(2):
            for r in range(ROWS):
                load(who, r).start()
        for c in copies:
            c.wait()
        for mine in (True, False):
            who, tab, to = (0, tab_ref, p_own) if mine else (1, sib_tab_ref, p_sib)
            base = (out_at if mine else out_at ^ 1) * ROWS
            side = core if mine else 1 - core
            sem = psems.at[who]

            def row(r, _, who=who, base=base, side=side, tab=tab, to=to, sem=sem):
                panels = []
                for k in range(KD1):
                    at = pl.ds(pl.multiple_of(cols_ref[base + r, k] * BLK, BLK), BLK)
                    pltpu.make_async_copy(whole.at[:, at], to.at[r, k], sem).start()
                    panels.append(whole[:, at] * (k < tab[r, 0]).astype(BF16))
                load(who, r).wait()
                weight = weights[who, r].reshape(KD1 * BLK, BLK)
                out = dot(jnp.concatenate(panels, axis=1), weight, ((1,), (0,)))
                out_ref[2 * r, side] = out[:, :SUB].astype(BF16)
                out_ref[2 * r + 1, side] = out[:, SUB:].astype(BF16)
                return 0

            lax.fori_loop(0, ROWS, row, 0)
        for mine in (True, False):
            to = p_own if mine else p_sib
            pltpu.make_async_copy(to, to, psems.at[0 if mine else 1]).wait()

    panels = pltpu.HBM((ROWS, KD1, frames, BLK), BF16)
    return pl.pallas_call(
        body,
        out_shape=(jax.ShapeDtypeStruct((2 * ROWS, 2, frames, SUB), BF16), panels, panels),
        in_specs=[SMEM] * 4 + [HBM] * (n + 2),
        out_specs=(VMEM, HBM, HBM),
        scratch_shapes=[
            pltpu.VMEM((frames, width), BF16),
            pltpu.VMEM((2, ROWS, KD1, BLK, BLK), BF16),
            pltpu.SemaphoreType.DMA((n_copies,)),
            pltpu.SemaphoreType.DMA((2, ROWS)),
            pltpu.SemaphoreType.DMA((2,)),
        ],
        compiler_params=limit(20),
        cost_estimate=pl.CostEstimate(flops=2**31, bytes_accessed=2**24, transcendentals=0),
        name="forward_first",
    )(pos, cols, table, sib_table, *in_hbm(*arrays, weight, sibling))


def relative(block, x, z):
    return (block // NZ - x) % NX * NZ + (block % NZ - z) % NZ


def forward_second(pos, table, sib_table, pieces, weight, sibling):
    frames = pieces[0].shape[2]

    def body(pos_ref, tab_ref, sib_tab_ref, *refs):
        srcs, (own_ref, sib_ref, out_ref, p_own, p_sib) = refs[:NX], refs[NX : NX + 5]
        blocks, panels, psems = refs[NX + 5 :]
        x, z, core = pos_ref[0], pos_ref[1], pos_ref[2]
        for k in range(NX):
            for zr in range(NZ):
                blocks[k * NZ + zr, :, :SUB] = srcs[k][zr, 0]
                blocks[k * NZ + zr, :, SUB:] = srcs[k][zr, 1]
        for mine in (True, False):
            w_ref, tab, to = (own_ref, tab_ref, p_own) if mine else (sib_ref, sib_tab_ref, p_sib)
            side = core if mine else 1 - core
            n = 0 if mine else 1

            def row(r, _):
                used = []
                for k in range(KD2):
                    panel = blocks[relative(tab[r, 2 + k], x, z)]
                    panels[n, r, k] = panel
                    used.append(panel * (k < tab[r, 1]).astype(BF16))
                pltpu.make_async_copy(panels.at[n, r], to.at[r], psems.at[n]).start()
                out = dot(jnp.concatenate(used, axis=1), w_ref[r].reshape(KD2 * BLK, BLK), ((1,), (0,)))
                out_ref[2 * r, side] = out[:, :SUB].astype(BF16)
                out_ref[2 * r + 1, side] = out[:, SUB:].astype(BF16)
                return 0

            lax.fori_loop(0, ROWS, row, 0)
        for n, to in enumerate((p_own, p_sib)):
            pltpu.make_async_copy(to, to, psems.at[n]).wait()

    panels = pltpu.HBM((ROWS, KD2, frames, BLK), BF16)
    return pl.pallas_call(
        body,
        out_shape=(jax.ShapeDtypeStruct((2 * ROWS, 2, frames, SUB), BF16), panels, panels),
        in_specs=[SMEM] * 3 + [VMEM] * (NX + 2),
        out_specs=(VMEM, HBM, HBM),
        scratch_shapes=[
            pltpu.VMEM((NX * NZ, frames, BLK), BF16),
            pltpu.VMEM((2, ROWS, KD2, frames, BLK), BF16),
            pltpu.SemaphoreType.DMA((2,)),
        ],
        compiler_params=limit(12),
        cost_estimate=pl.CostEstimate(flops=2**30, bytes_accessed=2**23, transcendentals=0),
        name="forward_second",
    )(pos, table, sib_table, *on_chip(*pieces, weight, sibling))


def adjoint_second(pos, table, sib_table, delta, weight, sibling):
    frames = delta.shape[2]

    def body(pos_ref, tab_ref, sib_tab_ref, d_ref, own_ref, sib_ref, *refs):
        outs, (acc,) = refs[:NX], refs[NX:]
        x, z, core = pos_ref[0], pos_ref[1], pos_ref[2]
        acc[...] = jnp.zeros(acc.shape, F32)
        for mine in (True, False):
            w_ref, tab = (own_ref, tab_ref) if mine else (sib_ref, sib_tab_ref)
            side = core if mine else 1 - core

            def row(r, _):
                d = halves(d_ref, r, side)
                terms = dot(d, w_ref[r].reshape(KD2 * BLK, BLK), ((1,), (1,)))
                for k in range(KD2):
                    term = terms[:, k * BLK : (k + 1) * BLK]
                    acc[relative(tab[r, 2 + k], x, z)] += term * (k < tab[r, 1]).astype(F32)
                return 0

            lax.fori_loop(0, ROWS, row, 0)
        for k in range(NX):
            for zr in range(NZ):
                outs[k][zr, 0] = acc[k * NZ + zr, :, :SUB].astype(BF16)
                outs[k][zr, 1] = acc[k * NZ + zr, :, SUB:].astype(BF16)

    return pl.pallas_call(
        body,
        out_shape=(jax.ShapeDtypeStruct((NZ, 2, frames, SUB), BF16),) * NX,
        in_specs=[SMEM] * 3 + [VMEM] * 3,
        out_specs=(VMEM,) * NX,
        scratch_shapes=[pltpu.VMEM((NX * NZ, frames, BLK), F32)],
        compiler_params=limit(12),
        cost_estimate=pl.CostEstimate(flops=2**30, bytes_accessed=2**23, transcendentals=0),
        name="adjoint_second",
    )(pos, table, sib_table, *on_chip(delta, weight, sibling))


def add_shares(parts):
    n = parts[0].shape[0]

    def body(*refs):
        ins, outs = refs[: len(parts)], refs[len(parts) :]
        for k in range(n):
            total = ins[0][k].astype(F32)
            for p in ins[1:]:
                total += p[k].astype(F32)
            outs[k][...] = total.astype(BF16)

    return pl.pallas_call(
        body,
        out_shape=(jax.ShapeDtypeStruct(parts[0].shape[1:], BF16),) * n,
        in_specs=[VMEM] * len(parts),
        out_specs=(VMEM,) * n,
        compiler_params=limit(8),
        name="add_shares",
    )(*on_chip(*parts))


def weight_grads(pos, table, field, panels, other_panels, deltas, name):
    arrays, rows_of = deltas
    slots, frames = panels.shape[1], panels.shape[2]

    def body(pos_ref, tab_ref, p_ref, po_ref, *refs):
        d_refs, (out_ref, grads, gsem) = refs[: len(arrays)], refs[len(arrays) :]
        core = pos_ref[2]

        def row(r, _):
            d = jnp.concatenate(rows_of(core, d_refs, r), axis=0)
            for k in range(slots):
                panel = jnp.concatenate([p_ref[r, k], po_ref[r, k]], axis=0)
                live = (k < tab_ref[r, field]).astype(F32)
                grads[r, k] = (dot(panel, d, ((0,), (0,))) * live).astype(BF16)
            pltpu.make_async_copy(grads.at[r], out_ref.at[r], gsem).start()
            return 0

        lax.fori_loop(0, ROWS, row, 0)
        pltpu.make_async_copy(out_ref, out_ref, gsem).wait()

    return pl.pallas_call(
        body,
        out_shape=jax.ShapeDtypeStruct((ROWS, slots, BLK, BLK), BF16),
        in_specs=[SMEM, SMEM] + [VMEM] * (2 + len(arrays)),
        out_specs=HBM,
        scratch_shapes=[
            pltpu.VMEM((ROWS, slots, BLK, BLK), BF16),
            pltpu.SemaphoreType.DMA,
        ],
        compiler_params=limit(12),
        cost_estimate=pl.CostEstimate(
            flops=slots * 2**27, bytes_accessed=slots * 2**20, transcendentals=0
        ),
        name=name,
    )(pos, table, *on_chip(panels, other_panels, *arrays))


def ring(value, axis, step, label="ring"):
    n = lax.axis_size(axis)
    with jax.named_scope("L_" + label):
        return lax.ppermute(value, axis, [(i, (i + step) % n) for i in range(n)])


def swap(value, label="swap"):
    with jax.named_scope("L_" + label):
        return lax.ppermute(value, "core", [(0, 1), (1, 0)])


def together(*values):
    return lax.optimization_barrier(values)


def gather_slopes(s, early):
    half = s.shape[1] // 2
    zp, zn = ring(s, "zh", 1, "zp"), ring(s, "zh", -1, "zn")
    xp, xn = ring(s, "x", 1, "xp"), ring(s, "x", -1, "xn")
    xp, xn = together(xp, xn)
    xl, xh = ring(xp[:, :half], "x", 1, "xl"), ring(xn[:, half:], "x", -1, "xh")
    zp, zn, xl, xh, early = together(zp, zn, xl, xh, early)
    zps, zns = zp[:, :half], zn[:, half:]
    t = jnp.concatenate([zp, zn], axis=0)
    zps, zns, t = together(zps, zns, t)
    zl, zr = ring(zps, "zh", 1, "zl"), ring(zns, "zh", -1, "zr")
    tp, tn = ring(t, "x", 1, "tp"), ring(t, "x", -1, "tn")
    w = jnp.concatenate([xl, xh], axis=1)
    zl, zr, w = together(zl, zr, w)
    wp, wn = ring(w, "zh", 1, "wp"), ring(w, "zh", -1, "wn")
    f = jnp.concatenate([zl, zr], axis=1)
    f, tp, tn = together(f, tp, tn)
    fp, fn = ring(f, "x", 1, "fp"), ring(f, "x", -1, "fn")
    fp, fn, wp, wn = together(fp, fn, wp, wn)
    fl, fh = ring(fp[:, :half], "x", 1, "fl"), ring(fn[:, half:], "x", -1, "fh")
    pieces = [(s, [(0, 0)], 0), (xp, [(-1, 0)], 0), (xn, [(1, 0)], 0), (w, [(2, 0)], 0)]
    pieces += [(t, [(0, -1), (0, 1)], 0), (tp, [(-1, -1), (-1, 1)], 0), (tn, [(1, -1), (1, 1)], 0)]
    pieces += [(wp, [(2, -1)], 0), (wn, [(2, 1)], 0)]
    pieces += [(f, [(0, 2)], 0), (fp, [(-1, 2)], 0), (fn, [(1, 2)], 0)]
    pieces += [(fl, [(2, 2)], 0), (fh, [(2, 2)], half)]
    return pieces, early


def gather_axis(value, axis):
    n = lax.axis_size(axis)
    return lax.all_to_all(jnp.broadcast_to(value[None], (n, *value.shape)), axis, 0, 0, tiled=True)


def sum_axis(parts, axis):
    return jnp.sum(lax.all_to_all(parts, axis, 0, 0, tiled=True).astype(F32), axis=0)


def shards(
    slopes,
    cols_first,
    count_first,
    weight_first,
    bias_first,
    cols_second,
    count_second,
    weight_second,
    bias_second,
    cotangent,
):
    frames = cotangent.shape[0]
    chips = NX * NZ
    own = slopes.shape[0]
    core = lax.axis_index("core")
    pos = jnp.stack(
        [lax.axis_index("x"), lax.axis_index("zh"), core, lax.axis_index(OUT)]
    ).astype(jnp.int32)

    def canonical(mine, other):
        return jnp.where(core == 0, jnp.stack([mine, other]), jnp.stack([other, mine]))

    pieces, sibling_first = gather_slopes(slopes, swap(weight_first, "w1"))
    sibling_second = swap(weight_second)
    table = jnp.concatenate([count_first, count_second, cols_second], axis=1)
    sib_table = swap(table)
    bias = jnp.stack([bias_first, bias_second])
    biases = canonical(bias, swap(bias))
    by_core = cotangent.reshape(chips, 2, own, SUB)
    mine = lax.dynamic_index_in_dim(by_core, core, 1, keepdims=False)
    theirs = lax.dynamic_index_in_dim(by_core, 1 - core, 1, keepdims=False)
    cot = canonical(mine, swap(theirs)).reshape(2, chips * own, SUB).astype(F32)

    partial_first, panels_first, lent_first = forward_first(
        pos, cols_first, table, sib_table, pieces, weight_first, sibling_first
    )
    summed_first = sum_axis(partial_first, IN)
    hidden_first = jnp.tanh(summed_first + biases[:, 0][:, None, :]).astype(BF16)
    along_z = jnp.stack([hidden_first] + [ring(hidden_first, "zh", -k) for k in range(1, NZ)])
    hidden = [along_z] + [ring(along_z, "x", -k) for k in range(1, NX)]

    partial_second, panels_second, lent_second = forward_second(
        pos, table, sib_table, hidden, weight_second, sibling_second
    )
    summed_second = sum_axis(partial_second, IN)
    estimate = jnp.tanh(summed_second + biases[:, 1][:, None, :]).astype(BF16)
    est32 = estimate.astype(F32)
    delta_second = (cot * (1.0 - est32 * est32)).astype(BF16)
    rows_second = gather_axis(delta_second, IN)

    back = adjoint_second(pos, table, sib_table, rows_second, weight_second, sibling_second)
    along_x = add_shares([back[0]] + [ring(back[k], "x", k) for k in range(1, NX)])
    shares = [along_x[0]] + [ring(along_x[k], "zh", k) for k in range(1, NZ)]
    back_first = sum(s.astype(F32) for s in shares)
    hid32 = hidden_first.astype(F32)
    delta_first = (back_first * (1.0 - hid32 * hid32)).astype(BF16)
    to_all = jnp.broadcast_to(delta_first[:, None], (2, lax.axis_size(IN), *delta_first.shape[1:]))
    rows_first = lax.all_to_all(
        to_all.reshape(-1, *delta_first.shape[1:]), ("core", *IN), 0, 0, tiled=True
    ).reshape(to_all.shape)
    lent_rows = swap(lax.dynamic_index_in_dim(rows_second, 1 - core, 1, keepdims=False))
    grad_second = weight_grads(
        pos,
        table,
        1,
        panels_second,
        swap(lent_second),
        (
            (rows_second, lent_rows),
            lambda core, refs, r: [halves(refs[0], r, core), halves(refs[1], r)],
        ),
        "grad_second",
    )
    est_own = lax.dynamic_index_in_dim(estimate, core, 0, keepdims=False)
    est_other = swap(lax.dynamic_index_in_dim(estimate, 1 - core, 0, keepdims=False))
    both = canonical(est_own, est_other).reshape(2, chips, own, SUB)
    estimate_out = both.transpose(1, 0, 2, 3).reshape(frames, SUB)
    rows_first, grad_second, estimate_out = together(rows_first, grad_second, estimate_out)
    grad_first = weight_grads(
        pos,
        table,
        0,
        panels_first,
        swap(lent_first),
        (
            (rows_first,),
            lambda core, refs, r: [halves(refs[0].at[core], r), halves(refs[0].at[1 - core], r)],
        ),
        "grad_first",
    )
    return (estimate_out, grad_first, grad_second)


def solution(mesh):
    fine = Mesh(mesh.devices.reshape(NX, NZ, 2, 2, 4), OUT + IN)
    return jax.shard_map(
        shards,
        mesh=fine,
        in_specs=(
            P(OUT, IN),
            P(None, IN),
            P(OUT, IN),
            P(OUT, IN, None, None),
            P(OUT + IN),
            P(OUT, IN),
            P(OUT, IN),
            P(OUT, IN, None, None),
            P(OUT + IN),
            P(None, OUT + IN),
        ),
        out_specs=(P(None, OUT + IN), P(OUT, IN, None, None), P(OUT, IN, None, None)),
        check_vma=False,
    )
```

```python
import jax
import jax.numpy as jnp
from jax import lax
from jax.experimental import pallas as pl
from jax.experimental.pallas import tpu as pltpu
from jax.sharding import Mesh
from jax.sharding import PartitionSpec as P

BLK = 256
KD1 = 8
KD2 = 4
SUB = 128
ROWS = 4
NX = 4
NZ = 4
CHUNK = 2560
OUT = ("x", "zh", "core")
IN = ("zl", "y")
F32 = jnp.float32
BF16 = jnp.bfloat16

HBM = pl.BlockSpec(memory_space=pltpu.HBM)
SMEM = pl.BlockSpec(memory_space=pltpu.SMEM)
VMEM = pl.BlockSpec(memory_space=pltpu.VMEM)


def dot(a, b, dims):
    return lax.dot_general(a, b, (dims, ((), ())), preferred_element_type=F32)


def halves(ref, row, *at):
    return jnp.concatenate([ref[(2 * row, *at)], ref[(2 * row + 1, *at)]], axis=1)


def limit(mib):
    return pltpu.CompilerParams(vmem_limit_bytes=mib * 2**20)


def on_chip(*values):
    return [pltpu.with_memory_space_constraint(v, pltpu.VMEM) for v in values]


def in_hbm(*values):
    return [pltpu.with_memory_space_constraint(v, pltpu.HBM) for v in values]


def forward_first(pos, cols, table, sib_table, pieces, weight, sibling):
    arrays = [a for a, _, _ in pieces]
    n = len(arrays)
    own_rows = arrays[0].shape[0]
    width = arrays[0].shape[1]
    frames = NX * NZ * own_rows
    n_copies = sum(len(o) for _, o, _ in pieces)

    def body(pos_ref, cols_ref, tab_ref, sib_tab_ref, *refs):
        srcs, (own_ref, sib_ref, out_ref, p_own, p_sib) = refs[:n], refs[n : n + 5]
        whole, weights, sems, wsems, psems = refs[n + 5 :]
        x, z, core, out_at = pos_ref[0], pos_ref[1], pos_ref[2], pos_ref[3]
        copies = []
        for src, (a, offsets, first) in zip(srcs, pieces):
            for m, (dx, dz) in enumerate(offsets):
                row = ((x + dx) % NX * NZ + (z + dz) % NZ) * own_rows
                for q in range(0, a.shape[1], CHUNK):
                    pltpu.make_async_copy(
                        src.at[pl.ds(m * own_rows, own_rows), pl.ds(q, CHUNK)],
                        whole.at[
                            pl.ds(pl.multiple_of(row, own_rows), own_rows),
                            pl.ds(first + q, CHUNK),
                        ],
                        sems.at[len(copies)],
                    ).start()
                copies.append(
                    pltpu.make_async_copy(
                        src.at[pl.ds(m * own_rows, own_rows), :],
                        whole.at[
                            pl.ds(pl.multiple_of(row, own_rows), own_rows),
                            pl.ds(first, a.shape[1]),
                        ],
                        sems.at[len(copies)],
                    )
                )

        def load(who, r):
            src = (own_ref, sib_ref)[who]
            return pltpu.make_async_copy(src.at[r], weights.at[who, r], wsems.at[who, r])

        load(0, 0).start()
        for c in copies:
            c.wait()
        for who in range(2):
            for r in range(ROWS):
                if who + r:
                    load(who, r).start()
        for mine in (True, False):
            who, tab, to = (0, tab_ref, p_own) if mine else (1, sib_tab_ref, p_sib)
            base = (out_at if mine else out_at ^ 1) * ROWS
            side = core if mine else 1 - core
            sem = psems.at[who]

            def row(r, _, who=who, base=base, side=side, tab=tab, to=to, sem=sem):
                panels = []
                for k in range(KD1):
                    at = pl.ds(pl.multiple_of(cols_ref[base + r, k] * BLK, BLK), BLK)
                    pltpu.make_async_copy(whole.at[:, at], to.at[r, k], sem).start()
                    panels.append(whole[:, at] * (k < tab[r, 0]).astype(BF16))
                load(who, r).wait()
                weight = weights[who, r].reshape(KD1 * BLK, BLK)
                out = dot(jnp.concatenate(panels, axis=1), weight, ((1,), (0,)))
                out_ref[2 * r, side] = out[:, :SUB].astype(BF16)
                out_ref[2 * r + 1, side] = out[:, SUB:].astype(BF16)
                return 0

            lax.fori_loop(0, ROWS, row, 0)
        for mine in (True, False):
            to = p_own if mine else p_sib
            pltpu.make_async_copy(to, to, psems.at[0 if mine else 1]).wait()

    panels = pltpu.HBM((ROWS, KD1, frames, BLK), BF16)
    return pl.pallas_call(
        body,
        out_shape=(jax.ShapeDtypeStruct((2 * ROWS, 2, frames, SUB), BF16), panels, panels),
        in_specs=[SMEM] * 4 + [HBM] * (n + 2),
        out_specs=(VMEM, HBM, HBM),
        scratch_shapes=[
            pltpu.VMEM((frames, width), BF16),
            pltpu.VMEM((2, ROWS, KD1, BLK, BLK), BF16),
            pltpu.SemaphoreType.DMA((n_copies,)),
            pltpu.SemaphoreType.DMA((2, ROWS)),
            pltpu.SemaphoreType.DMA((2,)),
        ],
        compiler_params=limit(20),
        cost_estimate=pl.CostEstimate(flops=2**31, bytes_accessed=2**24, transcendentals=0),
        name="forward_first",
    )(pos, cols, table, sib_table, *in_hbm(*arrays, weight, sibling))


def relative(block, x, z):
    return (block // NZ - x) % NX * NZ + (block % NZ - z) % NZ


def forward_second(pos, table, sib_table, pieces, weight, sibling):
    frames = pieces[0].shape[2]

    def body(pos_ref, tab_ref, sib_tab_ref, *refs):
        srcs, (own_ref, sib_ref, out_ref, p_own, p_sib) = refs[:NX], refs[NX : NX + 5]
        blocks, panels, psems = refs[NX + 5 :]
        x, z, core = pos_ref[0], pos_ref[1], pos_ref[2]
        for k in range(NX):
            for zr in range(NZ):
                blocks[k * NZ + zr, :, :SUB] = srcs[k][zr, 0]
                blocks[k * NZ + zr, :, SUB:] = srcs[k][zr, 1]
        for mine in (True, False):
            w_ref, tab, to = (own_ref, tab_ref, p_own) if mine else (sib_ref, sib_tab_ref, p_sib)
            side = core if mine else 1 - core
            n = 0 if mine else 1

            def row(r, _):
                used = []
                for k in range(KD2):
                    panel = blocks[relative(tab[r, 2 + k], x, z)]
                    panels[n, r, k] = panel
                    used.append(panel * (k < tab[r, 1]).astype(BF16))
                pltpu.make_async_copy(panels.at[n, r], to.at[r], psems.at[n]).start()
                out = dot(jnp.concatenate(used, axis=1), w_ref[r].reshape(KD2 * BLK, BLK), ((1,), (0,)))
                out_ref[2 * r, side] = out[:, :SUB].astype(BF16)
                out_ref[2 * r + 1, side] = out[:, SUB:].astype(BF16)
                return 0

            lax.fori_loop(0, ROWS, row, 0)
        for n, to in enumerate((p_own, p_sib)):
            pltpu.make_async_copy(to, to, psems.at[n]).wait()

    panels = pltpu.HBM((ROWS, KD2, frames, BLK), BF16)
    return pl.pallas_call(
        body,
        out_shape=(jax.ShapeDtypeStruct((2 * ROWS, 2, frames, SUB), BF16), panels, panels),
        in_specs=[SMEM] * 3 + [VMEM] * (NX + 2),
        out_specs=(VMEM, HBM, HBM),
        scratch_shapes=[
            pltpu.VMEM((NX * NZ, frames, BLK), BF16),
            pltpu.VMEM((2, ROWS, KD2, frames, BLK), BF16),
            pltpu.SemaphoreType.DMA((2,)),
        ],
        compiler_params=limit(12),
        cost_estimate=pl.CostEstimate(flops=2**30, bytes_accessed=2**23, transcendentals=0),
        name="forward_second",
    )(pos, table, sib_table, *on_chip(*pieces, weight, sibling))


def adjoint_second(pos, table, sib_table, delta, weight, sibling):
    frames = delta.shape[2]

    def body(pos_ref, tab_ref, sib_tab_ref, d_ref, own_ref, sib_ref, *refs):
        outs, (acc,) = refs[:NX], refs[NX:]
        x, z, core = pos_ref[0], pos_ref[1], pos_ref[2]
        acc[...] = jnp.zeros(acc.shape, F32)
        for mine in (True, False):
            w_ref, tab = (own_ref, tab_ref) if mine else (sib_ref, sib_tab_ref)
            side = core if mine else 1 - core

            def row(r, _):
                d = halves(d_ref, r, side)
                terms = dot(d, w_ref[r].reshape(KD2 * BLK, BLK), ((1,), (1,)))
                for k in range(KD2):
                    term = terms[:, k * BLK : (k + 1) * BLK]
                    acc[relative(tab[r, 2 + k], x, z)] += term * (k < tab[r, 1]).astype(F32)
                return 0

            lax.fori_loop(0, ROWS, row, 0)
        for k in range(NX):
            for zr in range(NZ):
                outs[k][zr, 0] = acc[k * NZ + zr, :, :SUB].astype(BF16)
                outs[k][zr, 1] = acc[k * NZ + zr, :, SUB:].astype(BF16)

    return pl.pallas_call(
        body,
        out_shape=(jax.ShapeDtypeStruct((NZ, 2, frames, SUB), BF16),) * NX,
        in_specs=[SMEM] * 3 + [VMEM] * 3,
        out_specs=(VMEM,) * NX,
        scratch_shapes=[pltpu.VMEM((NX * NZ, frames, BLK), F32)],
        compiler_params=limit(12),
        cost_estimate=pl.CostEstimate(flops=2**30, bytes_accessed=2**23, transcendentals=0),
        name="adjoint_second",
    )(pos, table, sib_table, *on_chip(delta, weight, sibling))


def add_shares(parts):
    n = parts[0].shape[0]

    def body(*refs):
        ins, outs = refs[: len(parts)], refs[len(parts) :]
        for k in range(n):
            total = ins[0][k].astype(F32)
            for p in ins[1:]:
                total += p[k].astype(F32)
            outs[k][...] = total.astype(BF16)

    return pl.pallas_call(
        body,
        out_shape=(jax.ShapeDtypeStruct(parts[0].shape[1:], BF16),) * n,
        in_specs=[VMEM] * len(parts),
        out_specs=(VMEM,) * n,
        compiler_params=limit(8),
        name="add_shares",
    )(*on_chip(*parts))


def weight_grads(pos, table, field, panels, other_panels, deltas, name):
    arrays, rows_of = deltas
    slots, frames = panels.shape[1], panels.shape[2]

    def body(pos_ref, tab_ref, p_ref, po_ref, *refs):
        d_refs, (out_ref, grads, gsem) = refs[: len(arrays)], refs[len(arrays) :]
        core = pos_ref[2]

        def row(r, _):
            d = jnp.concatenate(rows_of(core, d_refs, r), axis=0)
            for k in range(slots):
                panel = jnp.concatenate([p_ref[r, k], po_ref[r, k]], axis=0)
                live = (k < tab_ref[r, field]).astype(F32)
                grads[r, k] = (dot(panel, d, ((0,), (0,))) * live).astype(BF16)
            pltpu.make_async_copy(grads.at[r], out_ref.at[r], gsem).start()
            return 0

        lax.fori_loop(0, ROWS, row, 0)
        pltpu.make_async_copy(out_ref, out_ref, gsem).wait()

    return pl.pallas_call(
        body,
        out_shape=jax.ShapeDtypeStruct((ROWS, slots, BLK, BLK), BF16),
        in_specs=[SMEM, SMEM] + [VMEM] * (2 + len(arrays)),
        out_specs=HBM,
        scratch_shapes=[
            pltpu.VMEM((ROWS, slots, BLK, BLK), BF16),
            pltpu.SemaphoreType.DMA,
        ],
        compiler_params=limit(12),
        cost_estimate=pl.CostEstimate(
            flops=slots * 2**27, bytes_accessed=slots * 2**20, transcendentals=0
        ),
        name=name,
    )(pos, table, *on_chip(panels, other_panels, *arrays))


def ring(value, axis, step, label="ring"):
    n = lax.axis_size(axis)
    with jax.named_scope("L_" + label):
        return lax.ppermute(value, axis, [(i, (i + step) % n) for i in range(n)])


def swap(value, label="swap"):
    with jax.named_scope("L_" + label):
        return lax.ppermute(value, "core", [(0, 1), (1, 0)])


def together(*values):
    return lax.optimization_barrier(values)


def gather_slopes(s, early):
    half = s.shape[1] // 2
    zp, zn = ring(s, "zh", 1, "zp"), ring(s, "zh", -1, "zn")
    xp, xn = ring(s, "x", 1, "xp"), ring(s, "x", -1, "xn")
    xp, xn = together(xp, xn)
    xl, xh = ring(xp[:, :half], "x", 1, "xl"), ring(xn[:, half:], "x", -1, "xh")
    zp, zn, xl, xh, early = together(zp, zn, xl, xh, early)
    zps, zns = zp[:, :half], zn[:, half:]
    t = jnp.concatenate([zp, zn], axis=0)
    zps, zns, t = together(zps, zns, t)
    zl, zr = ring(zps, "zh", 1, "zl"), ring(zns, "zh", -1, "zr")
    tp, tn = ring(t, "x", 1, "tp"), ring(t, "x", -1, "tn")
    w = jnp.concatenate([xl, xh], axis=1)
    zl, zr, w = together(zl, zr, w)
    wp, wn = ring(w, "zh", 1, "wp"), ring(w, "zh", -1, "wn")
    f = jnp.concatenate([zl, zr], axis=1)
    f, tp, tn = together(f, tp, tn)
    fp, fn = ring(f, "x", 1, "fp"), ring(f, "x", -1, "fn")
    fp, fn, wp, wn = together(fp, fn, wp, wn)
    fl, fh = ring(fp[:, :half], "x", 1, "fl"), ring(fn[:, half:], "x", -1, "fh")
    pieces = [(s, [(0, 0)], 0), (xp, [(-1, 0)], 0), (xn, [(1, 0)], 0), (w, [(2, 0)], 0)]
    pieces += [(t, [(0, -1), (0, 1)], 0), (tp, [(-1, -1), (-1, 1)], 0), (tn, [(1, -1), (1, 1)], 0)]
    pieces += [(wp, [(2, -1)], 0), (wn, [(2, 1)], 0)]
    pieces += [(f, [(0, 2)], 0), (fp, [(-1, 2)], 0), (fn, [(1, 2)], 0)]
    pieces += [(fl, [(2, 2)], 0), (fh, [(2, 2)], half)]
    return pieces, early


def gather_axis(value, axis):
    n = lax.axis_size(axis)
    return lax.all_to_all(jnp.broadcast_to(value[None], (n, *value.shape)), axis, 0, 0, tiled=True)


def sum_axis(parts, axis):
    return jnp.sum(lax.all_to_all(parts, axis, 0, 0, tiled=True).astype(F32), axis=0)


def shards(
    slopes,
    cols_first,
    count_first,
    weight_first,
    bias_first,
    cols_second,
    count_second,
    weight_second,
    bias_second,
    cotangent,
):
    frames = cotangent.shape[0]
    chips = NX * NZ
    own = slopes.shape[0]
    core = lax.axis_index("core")
    pos = jnp.stack(
        [lax.axis_index("x"), lax.axis_index("zh"), core, lax.axis_index(OUT)]
    ).astype(jnp.int32)

    def canonical(mine, other):
        return jnp.where(core == 0, jnp.stack([mine, other]), jnp.stack([other, mine]))

    pieces, sibling_first = gather_slopes(slopes, swap(weight_first, "w1"))
    sibling_second = swap(weight_second)
    table = jnp.concatenate([count_first, count_second, cols_second], axis=1)
    sib_table = swap(table)
    bias = jnp.stack([bias_first, bias_second])
    biases = canonical(bias, swap(bias))
    by_core = cotangent.reshape(chips, 2, own, SUB)
    mine = lax.dynamic_index_in_dim(by_core, core, 1, keepdims=False)
    theirs = lax.dynamic_index_in_dim(by_core, 1 - core, 1, keepdims=False)
    cot = canonical(mine, swap(theirs)).reshape(2, chips * own, SUB).astype(F32)

    partial_first, panels_first, lent_first = forward_first(
        pos, cols_first, table, sib_table, pieces, weight_first, sibling_first
    )
    summed_first = sum_axis(partial_first, IN)
    hidden_first = jnp.tanh(summed_first + biases[:, 0][:, None, :]).astype(BF16)
    along_z = jnp.stack([hidden_first] + [ring(hidden_first, "zh", -k) for k in range(1, NZ)])
    hidden = [along_z] + [ring(along_z, "x", -k) for k in range(1, NX)]

    partial_second, panels_second, lent_second = forward_second(
        pos, table, sib_table, hidden, weight_second, sibling_second
    )
    summed_second = sum_axis(partial_second, IN)
    estimate = jnp.tanh(summed_second + biases[:, 1][:, None, :]).astype(BF16)
    est32 = estimate.astype(F32)
    delta_second = (cot * (1.0 - est32 * est32)).astype(BF16)
    rows_second = gather_axis(delta_second, IN)

    back = adjoint_second(pos, table, sib_table, rows_second, weight_second, sibling_second)
    along_x = add_shares([back[0]] + [ring(back[k], "x", k) for k in range(1, NX)])
    shares = [along_x[0]] + [ring(along_x[k], "zh", k) for k in range(1, NZ)]
    back_first = sum(s.astype(F32) for s in shares)
    hid32 = hidden_first.astype(F32)
    delta_first = (back_first * (1.0 - hid32 * hid32)).astype(BF16)
    to_all = jnp.broadcast_to(delta_first[:, None], (2, lax.axis_size(IN), *delta_first.shape[1:]))
    rows_first = lax.all_to_all(
        to_all.reshape(-1, *delta_first.shape[1:]), ("core", *IN), 0, 0, tiled=True
    ).reshape(to_all.shape)
    lent_rows = swap(lax.dynamic_index_in_dim(rows_second, 1 - core, 1, keepdims=False))
    grad_second = weight_grads(
        pos,
        table,
        1,
        panels_second,
        swap(lent_second),
        (
            (rows_second, lent_rows),
            lambda core, refs, r: [halves(refs[0], r, core), halves(refs[1], r)],
        ),
        "grad_second",
    )
    est_own = lax.dynamic_index_in_dim(estimate, core, 0, keepdims=False)
    est_other = swap(lax.dynamic_index_in_dim(estimate, 1 - core, 0, keepdims=False))
    both = canonical(est_own, est_other).reshape(2, chips, own, SUB)
    estimate_out = both.transpose(1, 0, 2, 3).reshape(frames, SUB)
    rows_first, grad_second, estimate_out = together(rows_first, grad_second, estimate_out)
    grad_first = weight_grads(
        pos,
        table,
        0,
        panels_first,
        swap(lent_first),
        (
            (rows_first,),
            lambda core, refs, r: [halves(refs[0].at[core], r), halves(refs[0].at[1 - core], r)],
        ),
        "grad_first",
    )
    return (estimate_out, grad_first, grad_second)


def solution(mesh):
    fine = Mesh(mesh.devices.reshape(NX, NZ, 2, 2, 4), OUT + IN)
    return jax.shard_map(
        shards,
        mesh=fine,
        in_specs=(
            P(OUT, IN),
            P(None, IN),
            P(OUT, IN),
            P(OUT, IN, None, None),
            P(OUT + IN),
            P(OUT, IN),
            P(OUT, IN),
            P(OUT, IN, None, None),
            P(OUT + IN),
            P(None, OUT + IN),
        ),
        out_specs=(P(None, OUT + IN), P(OUT, IN, None, None), P(OUT, IN, None, None)),
        check_vma=False,
    )
```

```python
import jax
import jax.numpy as jnp
from jax import lax
from jax.experimental import pallas as pl
from jax.experimental.pallas import tpu as pltpu
from jax.sharding import Mesh
from jax.sharding import PartitionSpec as P

BLK = 256
KD1 = 8
KD2 = 4
SUB = 128
ROWS = 4
NX = 4
NZ = 4
CHUNK = 2560
OUT = ("x", "zh", "core")
IN = ("zl", "y")
F32 = jnp.float32
BF16 = jnp.bfloat16

HBM = pl.BlockSpec(memory_space=pltpu.HBM)
SMEM = pl.BlockSpec(memory_space=pltpu.SMEM)
VMEM = pl.BlockSpec(memory_space=pltpu.VMEM)


def dot(a, b, dims):
    return lax.dot_general(a, b, (dims, ((), ())), preferred_element_type=F32)


def halves(ref, row, *at):
    return jnp.concatenate([ref[(2 * row, *at)], ref[(2 * row + 1, *at)]], axis=1)


def limit(mib):
    return pltpu.CompilerParams(vmem_limit_bytes=mib * 2**20)


def on_chip(*values):
    return [pltpu.with_memory_space_constraint(v, pltpu.VMEM) for v in values]


def in_hbm(*values):
    return [pltpu.with_memory_space_constraint(v, pltpu.HBM) for v in values]


def forward_first(pos, cols, table, sib_table, pieces, weight, sibling):
    arrays = [a for a, _, _ in pieces]
    n = len(arrays)
    own_rows = arrays[0].shape[0]
    width = arrays[0].shape[1]
    frames = NX * NZ * own_rows
    n_copies = sum(len(o) for _, o, _ in pieces)

    def body(pos_ref, cols_ref, tab_ref, sib_tab_ref, *refs):
        srcs, (own_ref, sib_ref, out_ref, p_own, p_sib) = refs[:n], refs[n : n + 5]
        whole, weights, sems, wsems, psems = refs[n + 5 :]
        x, z, core, out_at = pos_ref[0], pos_ref[1], pos_ref[2], pos_ref[3]
        copies = []
        for src, (a, offsets, first) in zip(srcs, pieces):
            for m, (dx, dz) in enumerate(offsets):
                row = ((x + dx) % NX * NZ + (z + dz) % NZ) * own_rows
                for q in range(0, a.shape[1], CHUNK):
                    pltpu.make_async_copy(
                        src.at[pl.ds(m * own_rows, own_rows), pl.ds(q, CHUNK)],
                        whole.at[
                            pl.ds(pl.multiple_of(row, own_rows), own_rows),
                            pl.ds(first + q, CHUNK),
                        ],
                        sems.at[len(copies)],
                    ).start()
                copies.append(
                    pltpu.make_async_copy(
                        src.at[pl.ds(m * own_rows, own_rows), :],
                        whole.at[
                            pl.ds(pl.multiple_of(row, own_rows), own_rows),
                            pl.ds(first, a.shape[1]),
                        ],
                        sems.at[len(copies)],
                    )
                )

        def load(who, r):
            src = (own_ref, sib_ref)[who]
            return pltpu.make_async_copy(src.at[r], weights.at[who, r], wsems.at[who, r])

        load(0, 0).start()
        for c in copies:
            c.wait()
        for who in range(2):
            for r in range(ROWS):
                if who + r:
                    load(who, r).start()
        for mine in (True, False):
            who, tab, to = (0, tab_ref, p_own) if mine else (1, sib_tab_ref, p_sib)
            base = (out_at if mine else out_at ^ 1) * ROWS
            side = core if mine else 1 - core
            sem = psems.at[who]

            def row(r, _, who=who, base=base, side=side, tab=tab, to=to, sem=sem):
                panels = []
                for k in range(KD1):
                    at = pl.ds(pl.multiple_of(cols_ref[base + r, k] * BLK, BLK), BLK)
                    pltpu.make_async_copy(whole.at[:, at], to.at[r, k], sem).start()
                    panels.append(whole[:, at] * (k < tab[r, 0]).astype(BF16))
                load(who, r).wait()
                weight = weights[who, r].reshape(KD1 * BLK, BLK)
                out = dot(jnp.concatenate(panels, axis=1), weight, ((1,), (0,)))
                out_ref[2 * r, side] = out[:, :SUB].astype(BF16)
                out_ref[2 * r + 1, side] = out[:, SUB:].astype(BF16)
                return 0

            lax.fori_loop(0, ROWS, row, 0)
        for mine in (True, False):
            to = p_own if mine else p_sib
            pltpu.make_async_copy(to, to, psems.at[0 if mine else 1]).wait()

    panels = pltpu.HBM((ROWS, KD1, frames, BLK), BF16)
    return pl.pallas_call(
        body,
        out_shape=(jax.ShapeDtypeStruct((2 * ROWS, 2, frames, SUB), BF16), panels, panels),
        in_specs=[SMEM] * 4 + [HBM] * (n + 2),
        out_specs=(VMEM, HBM, HBM),
        scratch_shapes=[
            pltpu.VMEM((frames, width), BF16),
            pltpu.VMEM((2, ROWS, KD1, BLK, BLK), BF16),
            pltpu.SemaphoreType.DMA((n_copies,)),
            pltpu.SemaphoreType.DMA((2, ROWS)),
            pltpu.SemaphoreType.DMA((2,)),
        ],
        compiler_params=limit(20),
        cost_estimate=pl.CostEstimate(flops=2**31, bytes_accessed=2**24, transcendentals=0),
        name="forward_first",
    )(pos, cols, table, sib_table, *in_hbm(*arrays, weight, sibling))


def relative(block, x, z):
    return (block // NZ - x) % NX * NZ + (block % NZ - z) % NZ


def forward_second(pos, table, sib_table, pieces, weight, sibling):
    frames = pieces[0].shape[2]

    def body(pos_ref, tab_ref, sib_tab_ref, *refs):
        srcs, (own_ref, sib_ref, out_ref, p_own, p_sib) = refs[:NX], refs[NX : NX + 5]
        blocks, panels, psems = refs[NX + 5 :]
        x, z, core = pos_ref[0], pos_ref[1], pos_ref[2]
        for k in range(NX):
            for zr in range(NZ):
                blocks[k * NZ + zr, :, :SUB] = srcs[k][zr, 0]
                blocks[k * NZ + zr, :, SUB:] = srcs[k][zr, 1]
        for mine in (True, False):
            w_ref, tab, to = (own_ref, tab_ref, p_own) if mine else (sib_ref, sib_tab_ref, p_sib)
            side = core if mine else 1 - core
            n = 0 if mine else 1

            def row(r, _):
                used = []
                for k in range(KD2):
                    panel = blocks[relative(tab[r, 2 + k], x, z)]
                    panels[n, r, k] = panel
                    used.append(panel * (k < tab[r, 1]).astype(BF16))
                pltpu.make_async_copy(panels.at[n, r], to.at[r], psems.at[n]).start()
                out = dot(jnp.concatenate(used, axis=1), w_ref[r].reshape(KD2 * BLK, BLK), ((1,), (0,)))
                out_ref[2 * r, side] = out[:, :SUB].astype(BF16)
                out_ref[2 * r + 1, side] = out[:, SUB:].astype(BF16)
                return 0

            lax.fori_loop(0, ROWS, row, 0)
        for n, to in enumerate((p_own, p_sib)):
            pltpu.make_async_copy(to, to, psems.at[n]).wait()

    panels = pltpu.HBM((ROWS, KD2, frames, BLK), BF16)
    return pl.pallas_call(
        body,
        out_shape=(jax.ShapeDtypeStruct((2 * ROWS, 2, frames, SUB), BF16), panels, panels),
        in_specs=[SMEM] * 3 + [VMEM] * (NX + 2),
        out_specs=(VMEM, HBM, HBM),
        scratch_shapes=[
            pltpu.VMEM((NX * NZ, frames, BLK), BF16),
            pltpu.VMEM((2, ROWS, KD2, frames, BLK), BF16),
            pltpu.SemaphoreType.DMA((2,)),
        ],
        compiler_params=limit(12),
        cost_estimate=pl.CostEstimate(flops=2**30, bytes_accessed=2**23, transcendentals=0),
        name="forward_second",
    )(pos, table, sib_table, *on_chip(*pieces, weight, sibling))


def adjoint_second(pos, table, sib_table, delta, weight, sibling):
    frames = delta.shape[2]

    def body(pos_ref, tab_ref, sib_tab_ref, d_ref, own_ref, sib_ref, *refs):
        outs, (acc,) = refs[:NX], refs[NX:]
        x, z, core = pos_ref[0], pos_ref[1], pos_ref[2]
        acc[...] = jnp.zeros(acc.shape, F32)
        for mine in (True, False):
            w_ref, tab = (own_ref, tab_ref) if mine else (sib_ref, sib_tab_ref)
            side = core if mine else 1 - core

            def row(r, _):
                d = halves(d_ref, r, side)
                terms = dot(d, w_ref[r].reshape(KD2 * BLK, BLK), ((1,), (1,)))
                for k in range(KD2):
                    term = terms[:, k * BLK : (k + 1) * BLK]
                    acc[relative(tab[r, 2 + k], x, z)] += term * (k < tab[r, 1]).astype(F32)
                return 0

            lax.fori_loop(0, ROWS, row, 0)
        for k in range(NX):
            for zr in range(NZ):
                outs[k][zr, 0] = acc[k * NZ + zr, :, :SUB].astype(BF16)
                outs[k][zr, 1] = acc[k * NZ + zr, :, SUB:].astype(BF16)

    return pl.pallas_call(
        body,
        out_shape=(jax.ShapeDtypeStruct((NZ, 2, frames, SUB), BF16),) * NX,
        in_specs=[SMEM] * 3 + [VMEM] * 3,
        out_specs=(VMEM,) * NX,
        scratch_shapes=[pltpu.VMEM((NX * NZ, frames, BLK), F32)],
        compiler_params=limit(12),
        cost_estimate=pl.CostEstimate(flops=2**30, bytes_accessed=2**23, transcendentals=0),
        name="adjoint_second",
    )(pos, table, sib_table, *on_chip(delta, weight, sibling))


def add_shares(parts):
    n = parts[0].shape[0]

    def body(*refs):
        ins, outs = refs[: len(parts)], refs[len(parts) :]
        for k in range(n):
            total = ins[0][k].astype(F32)
            for p in ins[1:]:
                total += p[k].astype(F32)
            outs[k][...] = total.astype(BF16)

    return pl.pallas_call(
        body,
        out_shape=(jax.ShapeDtypeStruct(parts[0].shape[1:], BF16),) * n,
        in_specs=[VMEM] * len(parts),
        out_specs=(VMEM,) * n,
        compiler_params=limit(8),
        name="add_shares",
    )(*on_chip(*parts))


def weight_grads(pos, table, field, panels, other_panels, deltas, name):
    arrays, rows_of = deltas
    slots, frames = panels.shape[1], panels.shape[2]

    def body(pos_ref, tab_ref, p_ref, po_ref, *refs):
        d_refs, (out_ref, grads, gsem) = refs[: len(arrays)], refs[len(arrays) :]
        core = pos_ref[2]

        def row(r, _):
            d = jnp.concatenate(rows_of(core, d_refs, r), axis=0)
            for k in range(slots):
                panel = jnp.concatenate([p_ref[r, k], po_ref[r, k]], axis=0)
                live = (k < tab_ref[r, field]).astype(F32)
                grads[r, k] = (dot(panel, d, ((0,), (0,))) * live).astype(BF16)
            pltpu.make_async_copy(grads.at[r], out_ref.at[r], gsem).start()
            return 0

        lax.fori_loop(0, ROWS, row, 0)
        pltpu.make_async_copy(out_ref, out_ref, gsem).wait()

    return pl.pallas_call(
        body,
        out_shape=jax.ShapeDtypeStruct((ROWS, slots, BLK, BLK), BF16),
        in_specs=[SMEM, SMEM] + [VMEM] * (2 + len(arrays)),
        out_specs=HBM,
        scratch_shapes=[
            pltpu.VMEM((ROWS, slots, BLK, BLK), BF16),
            pltpu.SemaphoreType.DMA,
        ],
        compiler_params=limit(12),
        cost_estimate=pl.CostEstimate(
            flops=slots * 2**27, bytes_accessed=slots * 2**20, transcendentals=0
        ),
        name=name,
    )(pos, table, *on_chip(panels, other_panels, *arrays))


def ring(value, axis, step, label="ring"):
    n = lax.axis_size(axis)
    with jax.named_scope("L_" + label):
        return lax.ppermute(value, axis, [(i, (i + step) % n) for i in range(n)])


def shares_of(values, axis, sign):
    far = ring(values[2], axis, 2, "far")
    one, three = ring(values[1], axis, sign, "one"), ring(values[3], axis, -sign, "three")
    far, one, three = together(far, one, three)
    return [values[0], one, far, three]


def swap(value, label="swap"):
    with jax.named_scope("L_" + label):
        return lax.ppermute(value, "core", [(0, 1), (1, 0)])


def together(*values):
    return lax.optimization_barrier(values)


def gather_slopes(s, early):
    half = s.shape[1] // 2
    zp, zn = ring(s, "zh", 1, "zp"), ring(s, "zh", -1, "zn")
    xp, xn = ring(s, "x", 1, "xp"), ring(s, "x", -1, "xn")
    xp, xn = together(xp, xn)
    xl, xh = ring(xp[:, :half], "x", 1, "xl"), ring(xn[:, half:], "x", -1, "xh")
    zp, zn, xl, xh, early = together(zp, zn, xl, xh, early)
    zps, zns = zp[:, :half], zn[:, half:]
    t = jnp.concatenate([zp, zn], axis=0)
    zps, zns, t = together(zps, zns, t)
    zl, zr = ring(zps, "zh", 1, "zl"), ring(zns, "zh", -1, "zr")
    tp, tn = ring(t, "x", 1, "tp"), ring(t, "x", -1, "tn")
    w = jnp.concatenate([xl, xh], axis=1)
    zl, zr, w = together(zl, zr, w)
    wp, wn = ring(w, "zh", 1, "wp"), ring(w, "zh", -1, "wn")
    f = jnp.concatenate([zl, zr], axis=1)
    f, tp, tn = together(f, tp, tn)
    fp, fn = ring(f, "x", 1, "fp"), ring(f, "x", -1, "fn")
    fp, fn, wp, wn = together(fp, fn, wp, wn)
    fl, fh = ring(fp[:, :half], "x", 1, "fl"), ring(fn[:, half:], "x", -1, "fh")
    pieces = [(s, [(0, 0)], 0), (xp, [(-1, 0)], 0), (xn, [(1, 0)], 0), (w, [(2, 0)], 0)]
    pieces += [(t, [(0, -1), (0, 1)], 0), (tp, [(-1, -1), (-1, 1)], 0), (tn, [(1, -1), (1, 1)], 0)]
    pieces += [(wp, [(2, -1)], 0), (wn, [(2, 1)], 0)]
    pieces += [(f, [(0, 2)], 0), (fp, [(-1, 2)], 0), (fn, [(1, 2)], 0)]
    pieces += [(fl, [(2, 2)], 0), (fh, [(2, 2)], half)]
    return pieces, early


def gather_axis(value, axis):
    n = lax.axis_size(axis)
    return lax.all_to_all(jnp.broadcast_to(value[None], (n, *value.shape)), axis, 0, 0, tiled=True)


def sum_axis(parts, axis):
    return jnp.sum(lax.all_to_all(parts, axis, 0, 0, tiled=True).astype(F32), axis=0)


def shards(
    slopes,
    cols_first,
    count_first,
    weight_first,
    bias_first,
    cols_second,
    count_second,
    weight_second,
    bias_second,
    cotangent,
):
    frames = cotangent.shape[0]
    chips = NX * NZ
    own = slopes.shape[0]
    core = lax.axis_index("core")
    pos = jnp.stack(
        [lax.axis_index("x"), lax.axis_index("zh"), core, lax.axis_index(OUT)]
    ).astype(jnp.int32)

    def canonical(mine, other):
        return jnp.where(core == 0, jnp.stack([mine, other]), jnp.stack([other, mine]))

    pieces, sibling_first = gather_slopes(slopes, swap(weight_first, "w1"))
    sibling_second = swap(weight_second)
    table = jnp.concatenate([count_first, count_second, cols_second], axis=1)
    sib_table = swap(table)
    bias = jnp.stack([bias_first, bias_second])
    biases = canonical(bias, swap(bias))
    by_core = cotangent.reshape(chips, 2, own, SUB)
    mine = lax.dynamic_index_in_dim(by_core, core, 1, keepdims=False)
    theirs = lax.dynamic_index_in_dim(by_core, 1 - core, 1, keepdims=False)
    cot = canonical(mine, swap(theirs)).reshape(2, chips * own, SUB).astype(F32)

    partial_first, panels_first, lent_first = forward_first(
        pos, cols_first, table, sib_table, pieces, weight_first, sibling_first
    )
    summed_first = sum_axis(partial_first, IN)
    hidden_first = jnp.tanh(summed_first + biases[:, 0][:, None, :]).astype(BF16)
    along_z = jnp.stack(shares_of([hidden_first] * NZ, "zh", -1))
    hidden = shares_of([along_z] * NX, "x", -1)

    partial_second, panels_second, lent_second = forward_second(
        pos, table, sib_table, hidden, weight_second, sibling_second
    )
    summed_second = sum_axis(partial_second, IN)
    estimate = jnp.tanh(summed_second + biases[:, 1][:, None, :]).astype(BF16)
    est32 = estimate.astype(F32)
    delta_second = (cot * (1.0 - est32 * est32)).astype(BF16)
    rows_second = gather_axis(delta_second, IN)

    back = adjoint_second(pos, table, sib_table, rows_second, weight_second, sibling_second)
    along_x = add_shares(shares_of(back, "x", 1))
    shares = shares_of(along_x, "zh", 1)
    back_first = sum(s.astype(F32) for s in shares)
    hid32 = hidden_first.astype(F32)
    delta_first = (back_first * (1.0 - hid32 * hid32)).astype(BF16)
    to_all = jnp.broadcast_to(delta_first[:, None], (2, lax.axis_size(IN), *delta_first.shape[1:]))
    rows_first = lax.all_to_all(
        to_all.reshape(-1, *delta_first.shape[1:]), ("core", *IN), 0, 0, tiled=True
    ).reshape(to_all.shape)
    lent_rows = swap(lax.dynamic_index_in_dim(rows_second, 1 - core, 1, keepdims=False))
    grad_second = weight_grads(
        pos,
        table,
        1,
        panels_second,
        swap(lent_second),
        (
            (rows_second, lent_rows),
            lambda core, refs, r: [halves(refs[0], r, core), halves(refs[1], r)],
        ),
        "grad_second",
    )
    est_own = lax.dynamic_index_in_dim(estimate, core, 0, keepdims=False)
    est_other = swap(lax.dynamic_index_in_dim(estimate, 1 - core, 0, keepdims=False))
    both = canonical(est_own, est_other).reshape(2, chips, own, SUB)
    estimate_out = both.transpose(1, 0, 2, 3).reshape(frames, SUB)
    rows_first, grad_second, estimate_out = together(rows_first, grad_second, estimate_out)
    grad_first = weight_grads(
        pos,
        table,
        0,
        panels_first,
        swap(lent_first),
        (
            (rows_first,),
            lambda core, refs, r: [halves(refs[0].at[core], r), halves(refs[0].at[1 - core], r)],
        ),
        "grad_first",
    )
    return (estimate_out, grad_first, grad_second)


def solution(mesh):
    fine = Mesh(mesh.devices.reshape(NX, NZ, 2, 2, 4), OUT + IN)
    return jax.shard_map(
        shards,
        mesh=fine,
        in_specs=(
            P(OUT, IN),
            P(None, IN),
            P(OUT, IN),
            P(OUT, IN, None, None),
            P(OUT + IN),
            P(OUT, IN),
            P(OUT, IN),
            P(OUT, IN, None, None),
            P(OUT + IN),
            P(None, OUT + IN),
        ),
        out_specs=(P(None, OUT + IN), P(OUT, IN, None, None), P(OUT, IN, None, None)),
        check_vma=False,
    )
```
